32 devices in a mesh: wa: 8 (over z, x), af: 4 (over y, core).
Axes of the slice: x: 2, y: 2, z: 4, core: 2. Of those that a mesh axis runs over, the one named last changes fastest.
Arguments:
- worker_ids: int32 [131072], P(('wa', 'af')), may hold values from 0 to 32767, as said below
- worker_attrs: bfloat16 [131072, 128], P(('wa', 'af')), may hold values from -16 to 16
- firm_ids: int32 [131072], P(('wa', 'af')), may hold values from 0 to 16383, as said below
- firm_attrs: bfloat16 [131072, 128], P(('wa', 'af')), may hold values from -16 to 16
- affinity: bfloat16 [128, 128], replicated, may hold values from -0.5 to 0.5
Outputs:
- worker_means: float32 [32768, 128], P('wa')
- firm_means: float32 [16384, 128], P('af')
- worker_potential: float32 [32768], P('wa')
- firm_potential: float32 [16384], P('af')
The draws below stay inside these ranges and needn't reach their ends.
Inputs may be any that keep to these rules, and one draw needn't show every extreme that they name: `worker_ids`: type ids come in blocks of 4096 consecutive worker types; in the rows of one device at most 1024 records name one block, and in every device's rows some block is named by exactly 1024. Counts per type are skewed and some types have no record. `firm_ids`: type ids come in blocks of 4096 consecutive firm types; in the rows of one device at most 2048 records name one block, and in every device's rows some block is named by exactly 2048. Counts per type are skewed and some types have no record.
All inputs are finite; a program needn't handle non-finite values.
Results may differ from the reference program's by a relative error of at most 0.00205.
The reference program's roundings to bfloat16 on the way (of `projected`) count: a program that leaves them out, or rounds other values in their place, can miss the bound.
Values may be sent and summed in bfloat16 or wider, within the bound.
A program may use at most 64 MiB of HBM per device.

```python
import math
import jax
import jax.numpy as jnp
from jax import lax

W = 32768
F = 16384
K = 128
R_DEV = 4096
ITERS = 3
WT_DEV = 4096
FT_DEV = 4096
RECORDS = 131072
CAP_W = 1024
CAP_F = 2048


def record_draw(key, salt, n_types, tile_types, capacity):
    key = jax.random.fold_in(key, salt)
    keys = jax.random.split(key, 7)
    groups = n_types // tile_types
    blocks = RECORDS // R_DEV
    heavy = jax.random.randint(keys[0], (blocks, 1), 0, groups)
    column = jnp.arange(R_DEV, dtype=jnp.int32)[None, :]
    spread = jnp.maximum(column - capacity, 0) % (groups - 1)
    owner = jnp.where(column < capacity, heavy, (heavy + 1 + spread) % groups)
    owner = jax.random.permutation(keys[1], owner, axis=1, independent=True)
    first = jax.random.randint(keys[2], (blocks, R_DEV), 0, tile_types)
    second = jax.random.randint(keys[3], (blocks, R_DEV), 0, tile_types)
    offset = jax.random.randint(keys[4], (groups,), 0, tile_types)
    slot = (jnp.minimum(first, second) + offset[owner]) % tile_types
    type_ids = (owner * tile_types + slot).reshape(RECORDS).astype(jnp.int32)
    centers = jax.random.normal(keys[5], (n_types, K), jnp.float32)
    noise = jax.random.normal(keys[6], (RECORDS, K), jnp.float32)
    return (type_ids, centers, noise)


def make_attrs(type_ids, centers, noise):
    scale = 0.5
    return jnp.clip(centers[type_ids] * scale + noise, -16.0, 16.0).astype(jnp.bfloat16)


def draw_worker_ids(key, part):
    type_ids, centers, noise = record_draw(key, 11, W, WT_DEV, CAP_W)
    return type_ids


def draw_worker_attrs(key, part):
    type_ids, centers, noise = record_draw(key, 11, W, WT_DEV, CAP_W)
    return make_attrs(type_ids, centers, noise)


def draw_firm_ids(key, part):
    type_ids, centers, noise = record_draw(key, 12, F, FT_DEV, CAP_F)
    return type_ids


def draw_firm_attrs(key, part):
    type_ids, centers, noise = record_draw(key, 12, F, FT_DEV, CAP_F)
    return make_attrs(type_ids, centers, noise)


def scatter_about(own_key, shape, scale, reach, kind=jnp.bfloat16):
    values = jax.random.normal(own_key, shape, jnp.float32) * scale
    return jnp.minimum(jnp.maximum(values, -reach), reach).astype(kind)


def setup_inputs(seed: int = 0) -> dict:
    key_list = jax.random.split(jax.random.key(seed), 6)
    worker_ids = draw_worker_ids(jax.random.fold_in(key_list[5], 71), 0)
    worker_attrs = draw_worker_attrs(jax.random.fold_in(key_list[5], 71), 0)
    firm_ids = draw_firm_ids(jax.random.fold_in(key_list[5], 71), 0)
    firm_attrs = draw_firm_attrs(jax.random.fold_in(key_list[5], 71), 0)
    affinity = scatter_about(key_list[4], (K, K), K ** -0.5, 0.5)
    return dict(worker_ids=worker_ids, worker_attrs=worker_attrs, firm_ids=firm_ids, firm_attrs=firm_attrs, affinity=affinity)


def type_means(attrs, type_ids, count):
    totals = jax.ops.segment_sum(attrs.astype(jnp.float32), type_ids, num_segments=count)
    tallies = jax.ops.segment_sum(jnp.ones(type_ids.shape, jnp.float32), type_ids, num_segments=count)
    return totals / jnp.maximum(tallies, 1.0)[:, None], tallies


def reference(worker_ids, worker_attrs, firm_ids, firm_attrs, affinity):
    worker_means, worker_tally = type_means(worker_attrs, worker_ids, W)
    firm_means, firm_tally = type_means(firm_attrs, firm_ids, F)
    log_worker = jnp.log(worker_tally + 1.0) - jnp.log(jnp.float32(RECORDS + W))
    log_firm = jnp.log(firm_tally + 1.0) - jnp.log(jnp.float32(RECORDS + F))
    projected = jnp.dot(worker_means.astype(jnp.bfloat16), affinity, preferred_element_type=jnp.float32).astype(jnp.bfloat16)
    projected = lax.optimization_barrier(projected).astype(jnp.float32)
    firm_rows = lax.optimization_barrier(firm_means.astype(jnp.bfloat16)).astype(jnp.float32)
    height = math.gcd(W, 512)
    stacked = projected.reshape(W // height, height, K)

    def surplus(rows_block):
        return jnp.dot(rows_block, firm_rows.T, precision=lax.Precision.HIGHEST, preferred_element_type=jnp.float32)

    firm_potential = jnp.zeros((F,), jnp.float32)
    worker_potential = jnp.zeros((W,), jnp.float32)
    for rounds in range(ITERS):
        def row_lse(rows_block, shift=firm_potential):
            scores = surplus(rows_block) + shift[None, :]
            peak = jnp.max(scores, axis=1)
            return peak + jnp.log(jnp.sum(jnp.exp(scores - peak[:, None]), axis=1))

        worker_potential = log_worker - lax.map(row_lse, stacked).reshape(W)

        def col_step(carry, inputs):
            peak, total = carry
            rows_block, shift_block = inputs
            scores = surplus(rows_block) + shift_block[:, None]
            new_peak = jnp.maximum(peak, jnp.max(scores, axis=0))
            total = total * jnp.exp(peak - new_peak) + jnp.sum(jnp.exp(scores - new_peak[None, :]), axis=0)
            return (new_peak, total), None

        start = (jnp.full((F,), -1e30, jnp.float32), jnp.zeros((F,), jnp.float32))
        (peak, total), unused = lax.scan(col_step, start, (stacked, worker_potential.reshape(W // height, height)))
        firm_potential = log_firm - (peak + jnp.log(total))
    return worker_means, firm_means, worker_potential, firm_potential
```

```python
import functools
import math

import jax
import jax.numpy as jnp
from jax import lax
from jax.experimental import pallas as pl
from jax.experimental.pallas import tpu as pltpu
from jax.sharding import PartitionSpec as P

W = 32768
F = 16384
ITERS = 3
LANES = 128
VMEM_BYTES = 60 * 1024 * 1024
MESH = pl.DeviceIdType.MESH


def select_kernel(chunk, wide, low_ref, sec_ref, attrs_ref, out_ref, rhs_ref):
    rows, width = attrs_ref.shape
    block = out_ref.shape[1]
    step = pl.program_id(0)

    @pl.when(step == 0)
    def _():
        eye = lax.broadcasted_iota(jnp.int32, (LANES, LANES), 0) == lax.broadcasted_iota(
            jnp.int32, (LANES, LANES), 1
        )

        def fill(c, carry):
            sec_row = jnp.broadcast_to(sec_ref[pl.ds(c, 1), :], (LANES, LANES))
            sec_col = jnp.sum(jnp.where(eye, sec_row, 0.0), axis=1, keepdims=True)
            spot = pl.ds(pl.multiple_of(c * LANES, LANES), LANES)
            part = attrs_ref[spot, :].astype(jnp.float32)
            for s in range(wide):
                rhs_ref[spot, s * width : (s + 1) * width] = jnp.where(
                    sec_col == s, part, 0.0
                ).astype(jnp.bfloat16)
            return carry

        lax.fori_loop(0, rows // LANES, fill, 0)

    target = lax.broadcasted_iota(jnp.int32, (block, chunk), 0) + step * block
    total = jnp.zeros((block, wide * width), jnp.float32)
    for c in range(rows // chunk):
        hit = jnp.where(low_ref[c : c + 1, :] == target, 1.0, 0.0).astype(jnp.bfloat16)
        total = total + jnp.dot(
            hit, rhs_ref[c * chunk : (c + 1) * chunk, :], preferred_element_type=jnp.float32
        )
    for s in range(wide):
        out_ref[s] = total[:, s * width : (s + 1) * width].astype(out_ref.dtype)


def select_sum(ids, attrs, count, dtype):
    rows, width = attrs.shape
    wide = 2
    span = count // wide
    block = math.gcd(span, 256)
    chunk = math.gcd(rows, 512)
    sec = ids // span
    low = (ids - sec * span).reshape(rows // chunk, chunk)
    sec = sec.astype(jnp.float32).reshape(rows // LANES, LANES)
    whole = lambda shape: pl.BlockSpec(shape, lambda i: (0,) * len(shape))
    out = pl.pallas_call(
        functools.partial(select_kernel, chunk, wide),
        grid=(span // block,),
        out_shape=jax.ShapeDtypeStruct((wide, span, width), dtype),
        in_specs=[whole(low.shape), whole(sec.shape), whole(attrs.shape)],
        out_specs=pl.BlockSpec((wide, block, width), lambda i: (0, i, 0)),
        scratch_shapes=[pltpu.VMEM((rows, wide * width), jnp.bfloat16)],
        compiler_params=pltpu.CompilerParams(vmem_limit_bytes=VMEM_BYTES),
        cost_estimate=pl.CostEstimate(
            flops=2 * rows * count * width, bytes_accessed=rows * width * 4, transcendentals=0
        ),
        name="select_sum",
    )(low, sec, attrs)
    return out.reshape(count, width)


def pack_records(type_ids, attrs, tile, groups, capacity):
    rows = type_ids.shape[0]
    owner = type_ids // tile
    local = type_ids - owner * tile
    grid = owner.reshape(rows // LANES, LANES)
    hits = (grid[None] == jnp.arange(groups, dtype=jnp.int32)[:, None, None])
    ramp = jnp.arange(LANES, dtype=jnp.int32)
    upper = (ramp[:, None] <= ramp[None, :]).astype(jnp.bfloat16)
    within = jnp.dot(hits.astype(jnp.bfloat16), upper, preferred_element_type=jnp.float32)
    lines = within[:, :, -1]
    line = jnp.arange(rows // LANES, dtype=jnp.int32)
    before = jnp.sum(
        jnp.where(line[None, :, None] < line[None, None, :], lines[:, :, None], 0.0), axis=1
    )
    rank = jnp.sum(jnp.where(hits, within - 1.0 + before[:, :, None], 0.0), axis=0)
    place = (grid * capacity + rank.astype(jnp.int32)).reshape(rows)
    sent_attrs = select_sum(place, attrs, groups * capacity, jnp.bfloat16)
    high, lowd = local // 64, local % 64
    filled = jnp.full((groups * capacity,), tile, jnp.int32)
    chosen = place_ids(place, jnp.stack([high, lowd, jnp.ones_like(high)]), groups, capacity)
    sent_ids = jnp.where(chosen[2] > 0.5, (chosen[0] * 64.0 + chosen[1]).astype(jnp.int32), filled)
    return (sent_attrs.reshape(groups, capacity, attrs.shape[1]), sent_ids.reshape(groups, capacity))


def place_ids(place, digits, groups, capacity):
    slots = groups * capacity
    high, low = place // LANES, place % LANES
    ahead = (high[None, :] == jnp.arange(slots // LANES, dtype=jnp.int32)[:, None])
    behind = (low[None, :] == jnp.arange(LANES, dtype=jnp.int32)[:, None]).astype(jnp.bfloat16)
    out = []
    for d in range(digits.shape[0]):
        left = jnp.where(ahead, digits[d][None, :].astype(jnp.bfloat16), jnp.bfloat16(0))
        out.append(
            lax.dot_general(left, behind, (((1,), (1,)), ((), ())), preferred_element_type=jnp.float32)
        )
    return jnp.stack(out).reshape(digits.shape[0], slots)


def pool_records(recv_attrs, recv_ids, tile):
    width = recv_attrs.shape[2]
    flat_ids = recv_ids.reshape(-1)
    totals = select_sum(flat_ids, recv_attrs.reshape(-1, width), tile, jnp.float32)
    high, low = flat_ids // LANES, flat_ids % LANES
    ahead = (high[None, :] == jnp.arange(tile // LANES, dtype=jnp.int32)[:, None])
    behind = (low[None, :] == jnp.arange(LANES, dtype=jnp.int32)[:, None])
    tallies = lax.dot_general(
        ahead.astype(jnp.bfloat16),
        behind.astype(jnp.bfloat16),
        (((1,), (1,)), ((), ())),
        preferred_element_type=jnp.float32,
    )
    return (totals, tallies.reshape(tile))


def joined(value, axis, combine):
    everything = jax.tree.map(lambda part: lax.all_gather(part, axis), value)
    initial = jax.tree.map(lambda part: part[0], everything)

    def step(k, so_far):
        return combine(so_far, jax.tree.map(lambda part: part[k], everything))

    return lax.fori_loop(1, lax.axis_size(axis), step, initial)


def merge_pair(left, right):
    peak = jnp.maximum(left[0], right[0])
    return (peak, left[1] * jnp.exp(left[0] - peak) + right[1] * jnp.exp(right[0] - peak))


def log_sweeps(projected, firm_rows, log_worker, log_firm):
    worker_tile, firm_tile = projected.shape[0], firm_rows.shape[0]
    height = math.gcd(worker_tile, 512)
    blocks = worker_tile // height

    def surplus(index):
        rows_block = lax.dynamic_slice_in_dim(projected, index * height, height, 0)
        return jnp.dot(rows_block, firm_rows.T, preferred_element_type=jnp.float32)

    def sweep(rounds, carry):
        firm_potential = carry[1]

        def row_stats(index):
            scores = surplus(index) + firm_potential[None, :]
            peak = jnp.max(scores, axis=1)
            return (peak, jnp.sum(jnp.exp(scores - peak[:, None]), axis=1))

        peak, total = lax.map(row_stats, jnp.arange(blocks, dtype=jnp.int32))
        peak, total = joined((peak.reshape(-1), total.reshape(-1)), "af", merge_pair)
        worker_potential = log_worker - (peak + jnp.log(total))

        def col_step(carry, inputs):
            peak, total = carry
            index, shift_block = inputs
            scores = surplus(index) + shift_block[:, None]
            new_peak = jnp.maximum(peak, jnp.max(scores, axis=0))
            total = total * jnp.exp(peak - new_peak) + jnp.sum(
                jnp.exp(scores - new_peak[None, :]), axis=0
            )
            return ((new_peak, total), None)

        start = (
            jnp.full((firm_tile,), -jnp.inf, jnp.float32),
            jnp.zeros((firm_tile,), jnp.float32),
        )
        (peak, total), _ = lax.scan(
            col_step,
            start,
            (jnp.arange(blocks, dtype=jnp.int32), worker_potential.reshape(blocks, height)),
        )
        peak, total = joined((peak, total), "wa", merge_pair)
        return (worker_potential, log_firm - (peak + jnp.log(total)))

    start = (jnp.zeros((worker_tile,), jnp.float32), jnp.zeros((firm_tile,), jnp.float32))
    return lax.fori_loop(0, ITERS, sweep, start)


TINY = 4e-28
LEAST = 1e-25
MOST = 1e30


def sweep_kernel(
    wa_size, af_size, proj_ref, firm_ref, wmass_ref, fmass_ref,
    wsum_ref, fsum_ref, bad_ref,
    e_ref, v_ref, u_ref, col_ref, msg_w, msg_f, msg_b, in_w, in_f, in_b,
    send_w, recv_w, send_f, recv_f, send_b, recv_b,
):
    wa, af = lax.axis_index("wa"), lax.axis_index("af")
    wt, ft = proj_ref.shape[0], firm_ref.shape[1]
    wr, fr = wt // LANES, ft // LANES

    barrier = pltpu.get_barrier_semaphore()
    for d in range(1, af_size):
        pl.semaphore_signal(
            barrier, inc=1, device_id=(wa, lax.rem(af + d, af_size)), device_id_type=MESH
        )
    for d in range(1, wa_size):
        pl.semaphore_signal(
            barrier, inc=1, device_id=(lax.rem(wa + d, wa_size), af), device_id_type=MESH
        )

    eye = lax.broadcasted_iota(jnp.int32, (LANES, LANES), 0) == lax.broadcasted_iota(
        jnp.int32, (LANES, LANES), 1
    )

    def lay(part):
        column = jnp.sum(part, axis=1, keepdims=True)
        return jnp.sum(jnp.where(eye, column, 0.0), axis=0, keepdims=True)

    def exchange(turn, msg, inbox, send, recv, size, along_af):
        copies = []
        for d in range(1, size):
            if along_af:
                peer = (wa, lax.rem(af + d, size))
            else:
                peer = (lax.rem(wa + d, size), af)
            slot = turn * (size - 1) + d - 1
            copies.append(
                pltpu.make_async_remote_copy(
                    src_ref=msg.at[turn],
                    dst_ref=inbox.at[slot],
                    send_sem=send.at[slot],
                    recv_sem=recv.at[slot],
                    device_id=peer,
                    device_id_type=MESH,
                )
            )
        for copy in copies:
            copy.start()
        for copy in copies:
            copy.wait()

    def ordered(turn, msg, inbox, size, me, rows):
        total = jnp.zeros((rows, LANES), jnp.float32)
        peak = jnp.zeros((8, LANES), jnp.float32)
        for k in range(size):
            d = lax.rem(me - k + size, size)
            slot = turn * (size - 1) + jnp.maximum(d - 1, 0)
            own = (d == 0).astype(jnp.float32) > 0.5
            value = jnp.where(own, msg[turn], inbox[slot])
            total = total + value[:rows]
            peak = jnp.maximum(peak, value[rows:])
        return total, peak

    def fill(b, carry):
        spot = pl.ds(pl.multiple_of(b * 256, 256), 256)
        acc = jnp.zeros((256, LANES), jnp.float32)
        for c in range(ft // 512):
            scores = jnp.dot(
                proj_ref[spot, :],
                firm_ref[:, c * 512 : (c + 1) * 512],
                preferred_element_type=jnp.float32,
            )
            grown = jnp.exp(scores)
            e_ref[spot, c * 512 : (c + 1) * 512] = grown.astype(jnp.bfloat16)
            for k in range(4):
                acc = acc + grown[:, k * LANES : (k + 1) * LANES]
        for k in range(2):
            msg_w[0, pl.ds(b * 2 + k, 1), :] = lay(acc[k * LANES : (k + 1) * LANES])
        return carry

    lax.fori_loop(0, wt // 256, fill, 0)
    pl.semaphore_wait(barrier, af_size + wa_size - 2)

    fault = jnp.zeros((8, LANES), jnp.float32)
    infinite = jnp.full((8, LANES), jnp.inf, jnp.float32)

    def row_pass(turn):
        def block(b, carry):
            spot = pl.ds(pl.multiple_of(b * LANES, LANES), LANES)
            acc = jnp.zeros((LANES, LANES), jnp.float32)
            for c in range(fr):
                acc = acc + e_ref[spot, c * LANES : (c + 1) * LANES].astype(
                    jnp.float32
                ) * v_ref[c : c + 1, :]
            msg_w[turn, pl.ds(b, 1), :] = lay(acc)
            return carry

        lax.fori_loop(0, wr, block, 0)

    def col_pass(turn):
        col_ref[...] = jnp.zeros_like(col_ref)

        def block(b, carry):
            spot = pl.ds(pl.multiple_of(b * LANES, LANES), LANES)
            row = jnp.broadcast_to(u_ref[pl.ds(b, 1), :], (LANES, LANES))
            scale = jnp.broadcast_to(
                jnp.sum(jnp.where(eye, row, 0.0), axis=1, keepdims=True), (LANES, LANES)
            )
            for c in range(fr):
                part = e_ref[spot, c * LANES : (c + 1) * LANES].astype(jnp.float32) * scale
                col_ref[c] += jnp.sum(part.reshape(LANES // 8, 8, LANES), axis=0)
            return carry

        lax.fori_loop(0, wr, block, 0)
        msg_f[turn, :fr, :] = jnp.sum(col_ref[...], axis=1)

    def judge(total, peak):
        least = jnp.min(total)
        most = jnp.max(total)
        good = (least > LEAST) & (most < MOST)
        fine = jnp.where(good, least, -1.0)
        return jnp.where(peak * TINY <= fine, 0.0, 1.0)

    for turn in range(ITERS):
        if turn == 0:
            biggest = jnp.ones((8, LANES), jnp.float32)
        else:
            row_pass(turn)
            biggest = jnp.full((8, LANES), jnp.max(v_ref[...]), jnp.float32)
        msg_w[turn, wr:, :] = jnp.where(fault > 0.5, infinite, biggest)
        exchange(turn, msg_w, in_w, send_w, recv_w, af_size, True)
        total, peak = ordered(turn, msg_w, in_w, af_size, af, wr)
        fault = judge(total, peak)
        u = wmass_ref[...] / total
        u_ref[...] = u
        if turn == ITERS - 1:
            wsum_ref[...] = total
        col_pass(turn)
        least_u = jnp.full((8, LANES), jnp.min(u), jnp.float32)
        spoiled = (fault > 0.5) | (least_u < 1e-35)
        msg_f[turn, fr:, :] = jnp.where(
            spoiled, infinite, jnp.full((8, LANES), jnp.max(u), jnp.float32)
        )
        exchange(turn, msg_f, in_f, send_f, recv_f, wa_size, False)
        total, peak = ordered(turn, msg_f, in_f, wa_size, wa, fr)
        fault = judge(total, peak)
        v_ref[...] = fmass_ref[...] / total
        if turn == ITERS - 1:
            fsum_ref[...] = total
    msg_b[0] = fault
    exchange(0, msg_b, in_b, send_b, recv_b, af_size, True)
    for d in range(1, af_size):
        fault = jnp.maximum(fault, in_b[d - 1])
    bad_ref[...] = fault


def fast_sweeps(projected, firm_rows, worker_mass, firm_mass):
    wa_size, af_size = lax.axis_size("wa"), lax.axis_size("af")
    wt, ft = projected.shape[0], firm_rows.shape[0]
    wr, fr = wt // LANES, ft // LANES
    vmem = pl.BlockSpec(memory_space=pltpu.VMEM)
    f32 = jnp.float32
    return pl.pallas_call(
        functools.partial(sweep_kernel, wa_size, af_size),
        out_shape=(
            jax.ShapeDtypeStruct((wr, LANES), f32),
            jax.ShapeDtypeStruct((fr, LANES), f32),
            jax.ShapeDtypeStruct((8, LANES), f32),
        ),
        in_specs=[vmem] * 4,
        out_specs=(vmem, vmem, vmem),
        scratch_shapes=[
            pltpu.VMEM((wt, ft), jnp.bfloat16),
            pltpu.VMEM((fr, LANES), f32),
            pltpu.VMEM((wr, LANES), f32),
            pltpu.VMEM((fr, 8, LANES), f32),
            pltpu.VMEM((ITERS, wr + 8, LANES), f32),
            pltpu.VMEM((ITERS, fr + 8, LANES), f32),
            pltpu.VMEM((1, 8, LANES), f32),
            pltpu.VMEM((ITERS * (af_size - 1), wr + 8, LANES), f32),
            pltpu.VMEM((ITERS * (wa_size - 1), fr + 8, LANES), f32),
            pltpu.VMEM((af_size - 1, 8, LANES), f32),
            pltpu.SemaphoreType.DMA((ITERS * (af_size - 1),)),
            pltpu.SemaphoreType.DMA((ITERS * (af_size - 1),)),
            pltpu.SemaphoreType.DMA((ITERS * (wa_size - 1),)),
            pltpu.SemaphoreType.DMA((ITERS * (wa_size - 1),)),
            pltpu.SemaphoreType.DMA((af_size - 1,)),
            pltpu.SemaphoreType.DMA((af_size - 1,)),
        ],
        compiler_params=pltpu.CompilerParams(
            collective_id=0, has_side_effects=True, vmem_limit_bytes=VMEM_BYTES
        ),
        name="sweeps",
    )(projected, firm_rows.T, worker_mass.reshape(wr, LANES), firm_mass.reshape(fr, LANES))


def body(worker_ids, worker_attrs, firm_ids, firm_attrs, affinity):
    rows = worker_ids.shape[0]
    wa_count = lax.axis_size("wa")
    af_count = lax.axis_size("af")
    worker_tile = W // wa_count
    firm_tile = F // af_count
    records_all = rows * wa_count * af_count
    sent_attrs, sent_ids = pack_records(
        worker_ids, worker_attrs, worker_tile, wa_count, 2 * rows // wa_count
    )
    recv_attrs = lax.all_to_all(sent_attrs, "wa", split_axis=0, concat_axis=0, tiled=True)
    recv_ids = lax.all_to_all(sent_ids, "wa", split_axis=0, concat_axis=0, tiled=True)
    worker_sum, worker_tally = pool_records(recv_attrs, recv_ids, worker_tile)
    sent_attrs, sent_ids = pack_records(
        firm_ids, firm_attrs, firm_tile, af_count, 2 * rows // af_count
    )
    recv_attrs = lax.all_to_all(sent_attrs, "af", split_axis=0, concat_axis=0, tiled=True)
    recv_ids = lax.all_to_all(sent_ids, "af", split_axis=0, concat_axis=0, tiled=True)
    firm_sum, firm_tally = pool_records(recv_attrs, recv_ids, firm_tile)
    worker_sum, worker_tally = lax.psum((worker_sum, worker_tally), "af")
    worker_means = worker_sum / jnp.maximum(worker_tally, 1.0)[:, None]
    firm_sum, firm_tally = lax.psum((firm_sum, firm_tally), "wa")
    firm_means = firm_sum / jnp.maximum(firm_tally, 1.0)[:, None]
    log_worker = jnp.log(worker_tally + 1.0) - jnp.log(jnp.float32(records_all + W))
    log_firm = jnp.log(firm_tally + 1.0) - jnp.log(jnp.float32(records_all + F))
    projected = jnp.dot(
        worker_means.astype(jnp.bfloat16), affinity, preferred_element_type=jnp.float32
    ).astype(jnp.bfloat16)
    firm_rows = firm_means.astype(jnp.bfloat16)
    worker_total, firm_total, bad = fast_sweeps(
        projected,
        firm_rows,
        (worker_tally + 1.0) / jnp.float32(records_all + W),
        (firm_tally + 1.0) / jnp.float32(records_all + F),
    )
    worker_potential, firm_potential = lax.cond(
        bad[0, 0] > 0.5,
        lambda: log_sweeps(projected, firm_rows, log_worker, log_firm),
        lambda: (
            log_worker - jnp.log(worker_total.reshape(-1)),
            log_firm - jnp.log(firm_total.reshape(-1)),
        ),
    )
    return (worker_means, firm_means, worker_potential, firm_potential)


def solution(mesh):
    placed = (P(("wa", "af")), P(("wa", "af"), None), P(("wa", "af")), P(("wa", "af"), None), P())
    return jax.shard_map(
        body,
        mesh=mesh,
        in_specs=placed,
        out_specs=(P("wa", None), P("af", None), P("wa"), P("af")),
        check_vma=False,
    )
```

```python
import functools
import math

import jax
import jax.numpy as jnp
from jax import lax
from jax.experimental import pallas as pl
from jax.experimental.pallas import tpu as pltpu
from jax.sharding import PartitionSpec as P

W = 32768
F = 16384
ITERS = 3
LANES = 128
VMEM_BYTES = 60 * 1024 * 1024
MESH = pl.DeviceIdType.MESH


def select_kernel(chunk, wide, low_ref, sec_ref, attrs_ref, out_ref, rhs_ref):
    rows, width = attrs_ref.shape
    block = out_ref.shape[1]
    step = pl.program_id(0)

    @pl.when(step == 0)
    def _():
        eye = lax.broadcasted_iota(jnp.int32, (LANES, LANES), 0) == lax.broadcasted_iota(
            jnp.int32, (LANES, LANES), 1
        )

        def fill(c, carry):
            sec_row = jnp.broadcast_to(sec_ref[pl.ds(c, 1), :], (LANES, LANES))
            sec_col = jnp.sum(jnp.where(eye, sec_row, 0.0), axis=1, keepdims=True)
            spot = pl.ds(pl.multiple_of(c * LANES, LANES), LANES)
            part = attrs_ref[spot, :].astype(jnp.float32)
            for s in range(wide):
                rhs_ref[spot, s * width : (s + 1) * width] = jnp.where(
                    sec_col == s, part, 0.0
                ).astype(jnp.bfloat16)
            return carry

        lax.fori_loop(0, rows // LANES, fill, 0)

    target = lax.broadcasted_iota(jnp.int32, (block, chunk), 0) + step * block
    total = jnp.zeros((block, wide * width), jnp.float32)
    for c in range(rows // chunk):
        hit = jnp.where(low_ref[c : c + 1, :] == target, 1.0, 0.0).astype(jnp.bfloat16)
        total = total + jnp.dot(
            hit, rhs_ref[c * chunk : (c + 1) * chunk, :], preferred_element_type=jnp.float32
        )
    for s in range(wide):
        out_ref[s] = total[:, s * width : (s + 1) * width].astype(out_ref.dtype)


def select_sum(ids, attrs, count, dtype):
    rows, width = attrs.shape
    wide = 2
    span = count // wide
    block = math.gcd(span, 256)
    chunk = math.gcd(rows, 512)
    sec = ids // span
    low = (ids - sec * span).reshape(rows // chunk, chunk)
    sec = sec.astype(jnp.float32).reshape(rows // LANES, LANES)
    whole = lambda shape: pl.BlockSpec(shape, lambda i: (0,) * len(shape))
    out = pl.pallas_call(
        functools.partial(select_kernel, chunk, wide),
        grid=(span // block,),
        out_shape=jax.ShapeDtypeStruct((wide, span, width), dtype),
        in_specs=[whole(low.shape), whole(sec.shape), whole(attrs.shape)],
        out_specs=pl.BlockSpec((wide, block, width), lambda i: (0, i, 0)),
        scratch_shapes=[pltpu.VMEM((rows, wide * width), jnp.bfloat16)],
        compiler_params=pltpu.CompilerParams(vmem_limit_bytes=VMEM_BYTES),
        cost_estimate=pl.CostEstimate(
            flops=2 * rows * count * width, bytes_accessed=rows * width * 4, transcendentals=0
        ),
        name="select_sum",
    )(low, sec, attrs)
    return out.reshape(count, width)


def pack_records(type_ids, attrs, tile, groups, capacity):
    rows = type_ids.shape[0]
    owner = type_ids // tile
    local = type_ids - owner * tile
    grid = owner.reshape(rows // LANES, LANES)
    hits = (grid[None] == jnp.arange(groups, dtype=jnp.int32)[:, None, None])
    ramp = jnp.arange(LANES, dtype=jnp.int32)
    upper = (ramp[:, None] <= ramp[None, :]).astype(jnp.bfloat16)
    within = jnp.dot(hits.astype(jnp.bfloat16), upper, preferred_element_type=jnp.float32)
    lines = within[:, :, -1]
    line = jnp.arange(rows // LANES, dtype=jnp.int32)
    before = jnp.sum(
        jnp.where(line[None, :, None] < line[None, None, :], lines[:, :, None], 0.0), axis=1
    )
    rank = jnp.sum(jnp.where(hits, within - 1.0 + before[:, :, None], 0.0), axis=0)
    place = (grid * capacity + rank.astype(jnp.int32)).reshape(rows)
    sent_attrs = select_sum(place, attrs, groups * capacity, jnp.bfloat16)
    high, lowd = local // 64, local % 64
    filled = jnp.full((groups * capacity,), tile, jnp.int32)
    chosen = place_ids(place, jnp.stack([high, lowd, jnp.ones_like(high)]), groups, capacity)
    sent_ids = jnp.where(chosen[2] > 0.5, (chosen[0] * 64.0 + chosen[1]).astype(jnp.int32), filled)
    return (sent_attrs.reshape(groups, capacity, attrs.shape[1]), sent_ids.reshape(groups, capacity))


def place_ids(place, digits, groups, capacity):
    slots = groups * capacity
    high, low = place // LANES, place % LANES
    ahead = (high[None, :] == jnp.arange(slots // LANES, dtype=jnp.int32)[:, None])
    behind = (low[None, :] == jnp.arange(LANES, dtype=jnp.int32)[:, None]).astype(jnp.bfloat16)
    out = []
    for d in range(digits.shape[0]):
        left = jnp.where(ahead, digits[d][None, :].astype(jnp.bfloat16), jnp.bfloat16(0))
        out.append(
            lax.dot_general(left, behind, (((1,), (1,)), ((), ())), preferred_element_type=jnp.float32)
        )
    return jnp.stack(out).reshape(digits.shape[0], slots)


def pool_records(recv_attrs, recv_ids, tile):
    width = recv_attrs.shape[2]
    flat_ids = recv_ids.reshape(-1)
    totals = select_sum(flat_ids, recv_attrs.reshape(-1, width), tile, jnp.float32)
    high, low = flat_ids // LANES, flat_ids % LANES
    ahead = (high[None, :] == jnp.arange(tile // LANES, dtype=jnp.int32)[:, None])
    behind = (low[None, :] == jnp.arange(LANES, dtype=jnp.int32)[:, None])
    tallies = lax.dot_general(
        ahead.astype(jnp.bfloat16),
        behind.astype(jnp.bfloat16),
        (((1,), (1,)), ((), ())),
        preferred_element_type=jnp.float32,
    )
    return (totals, tallies.reshape(tile))


def shared_means(sums, tally, axis):
    tile, width = sums.shape
    both = lax.psum(jnp.concatenate([sums, tally.reshape(tile // width, width)], axis=0), axis)
    tally = both[tile:].reshape(tile)
    return (both[:tile] / jnp.maximum(tally, 1.0)[:, None], tally)


def joined(value, axis, combine):
    everything = jax.tree.map(lambda part: lax.all_gather(part, axis), value)
    initial = jax.tree.map(lambda part: part[0], everything)

    def step(k, so_far):
        return combine(so_far, jax.tree.map(lambda part: part[k], everything))

    return lax.fori_loop(1, lax.axis_size(axis), step, initial)


def merge_pair(left, right):
    peak = jnp.maximum(left[0], right[0])
    return (peak, left[1] * jnp.exp(left[0] - peak) + right[1] * jnp.exp(right[0] - peak))


def log_sweeps(projected, firm_rows, log_worker, log_firm):
    worker_tile, firm_tile = projected.shape[0], firm_rows.shape[0]
    height = math.gcd(worker_tile, 512)
    blocks = worker_tile // height

    def surplus(index):
        rows_block = lax.dynamic_slice_in_dim(projected, index * height, height, 0)
        return jnp.dot(rows_block, firm_rows.T, preferred_element_type=jnp.float32)

    def sweep(rounds, carry):
        firm_potential = carry[1]

        def row_stats(index):
            scores = surplus(index) + firm_potential[None, :]
            peak = jnp.max(scores, axis=1)
            return (peak, jnp.sum(jnp.exp(scores - peak[:, None]), axis=1))

        peak, total = lax.map(row_stats, jnp.arange(blocks, dtype=jnp.int32))
        peak, total = joined((peak.reshape(-1), total.reshape(-1)), "af", merge_pair)
        worker_potential = log_worker - (peak + jnp.log(total))

        def col_step(carry, inputs):
            peak, total = carry
            index, shift_block = inputs
            scores = surplus(index) + shift_block[:, None]
            new_peak = jnp.maximum(peak, jnp.max(scores, axis=0))
            total = total * jnp.exp(peak - new_peak) + jnp.sum(
                jnp.exp(scores - new_peak[None, :]), axis=0
            )
            return ((new_peak, total), None)

        start = (
            jnp.full((firm_tile,), -jnp.inf, jnp.float32),
            jnp.zeros((firm_tile,), jnp.float32),
        )
        (peak, total), _ = lax.scan(
            col_step,
            start,
            (jnp.arange(blocks, dtype=jnp.int32), worker_potential.reshape(blocks, height)),
        )
        peak, total = joined((peak, total), "wa", merge_pair)
        return (worker_potential, log_firm - (peak + jnp.log(total)))

    start = (jnp.zeros((worker_tile,), jnp.float32), jnp.zeros((firm_tile,), jnp.float32))
    return lax.fori_loop(0, ITERS, sweep, start)


TINY = 4e-28
LEAST = 1e-25
MOST = 1e30


def sweep_kernel(
    wa_size, af_size, proj_ref, firm_ref, wmass_ref, fmass_ref,
    wsum_ref, fsum_ref, bad_ref,
    e_ref, s_ref, v_ref, u_ref, col_ref, msg_w, msg_f, msg_b, msg_m, in_w, in_f, in_b, in_m,
    send_w, recv_w, send_f, recv_f, send_b, recv_b, send_m, recv_m,
):
    wa, af = lax.axis_index("wa"), lax.axis_index("af")
    wt, ft = proj_ref.shape[0], firm_ref.shape[1]
    wr, fr = wt // LANES, ft // LANES

    barrier = pltpu.get_barrier_semaphore()
    for d in range(1, af_size):
        pl.semaphore_signal(
            barrier, inc=1, device_id=(wa, lax.rem(af + d, af_size)), device_id_type=MESH
        )
    for d in range(1, wa_size):
        pl.semaphore_signal(
            barrier, inc=1, device_id=(lax.rem(wa + d, wa_size), af), device_id_type=MESH
        )

    eye = lax.broadcasted_iota(jnp.int32, (LANES, LANES), 0) == lax.broadcasted_iota(
        jnp.int32, (LANES, LANES), 1
    )

    def lay(column):
        return jnp.sum(jnp.where(eye, column, 0.0), axis=0, keepdims=True)

    def exchange(turn, msg, inbox, send, recv, size, along_af):
        copies = []
        for d in range(1, size):
            if along_af:
                peer = (wa, lax.rem(af + d, size))
            else:
                peer = (lax.rem(wa + d, size), af)
            slot = turn * (size - 1) + d - 1
            copies.append(
                pltpu.make_async_remote_copy(
                    src_ref=msg.at[turn],
                    dst_ref=inbox.at[slot],
                    send_sem=send.at[slot],
                    recv_sem=recv.at[slot],
                    device_id=peer,
                    device_id_type=MESH,
                )
            )
        for copy in copies:
            copy.start()
        return copies

    def finish(copies):
        for copy in copies:
            copy.wait()

    def arrival(turn, msg, inbox, size, me, k):
        d = lax.rem(me - k + size, size)
        slot = turn * (size - 1) + jnp.maximum(d - 1, 0)
        return jnp.where(d == 0, msg[turn], inbox[slot])

    def ordered(turn, msg, inbox, size, me, rows, weights=None):
        total = jnp.zeros((rows, LANES), jnp.float32)
        peak = jnp.zeros((8, LANES), jnp.float32)
        for k in range(size):
            value = arrival(turn, msg, inbox, size, me, k)
            part = value[:rows]
            if weights is not None:
                part = part * weights[k]
            total = total + part
            peak = jnp.maximum(peak, value[rows:])
        return total, peak

    def fill(b, carry):
        spot = pl.ds(pl.multiple_of(b * 256, 256), 256)
        peak = jnp.full((256, LANES), -jnp.inf, jnp.float32)
        for c in range(ft // 512):
            scores = jnp.dot(
                proj_ref[spot, :],
                firm_ref[:, c * 512 : (c + 1) * 512],
                preferred_element_type=jnp.float32,
            )
            s_ref[:, c * 512 : (c + 1) * 512] = scores
            for k in range(4):
                peak = jnp.maximum(peak, scores[:, k * LANES : (k + 1) * LANES])
        peak = jnp.max(peak, axis=1, keepdims=True)
        shift = jnp.broadcast_to(peak, (256, LANES))
        acc = jnp.zeros((256, LANES), jnp.float32)
        for c in range(fr):
            grown = jnp.exp(s_ref[:, c * LANES : (c + 1) * LANES] - shift)
            e_ref[spot, c * LANES : (c + 1) * LANES] = grown.astype(jnp.bfloat16)
            acc = acc + grown
        total = jnp.sum(acc, axis=1, keepdims=True)
        for k in range(2):
            part = slice(k * LANES, (k + 1) * LANES)
            msg_w[0, pl.ds(b * 2 + k, 1), :] = lay(total[part])
            msg_m[0, pl.ds(b * 2 + k, 1), :] = lay(peak[part])
        return carry

    lax.fori_loop(0, wt // 256, fill, 0)
    pl.semaphore_wait(barrier, af_size + wa_size - 2)

    fault = jnp.zeros((8, LANES), jnp.float32)
    infinite = jnp.full((8, LANES), jnp.inf, jnp.float32)

    def row_pass(turn, scale):
        def block(b, carry):
            spot = pl.ds(pl.multiple_of(b * LANES, LANES), LANES)
            acc = jnp.zeros((LANES, LANES), jnp.float32)
            for c in range(fr):
                acc = acc + e_ref[spot, c * LANES : (c + 1) * LANES].astype(
                    jnp.float32
                ) * v_ref[c : c + 1, :]
            msg_w[turn, pl.ds(b, 1), :] = lay(jnp.sum(acc, axis=1, keepdims=True))
            return carry

        lax.fori_loop(0, wr, block, 0)
        msg_w[turn, :wr, :] = msg_w[turn, :wr, :] * scale

    def col_pass(turn):
        col_ref[...] = jnp.zeros_like(col_ref)

        def block(b, carry):
            spot = pl.ds(pl.multiple_of(b * LANES, LANES), LANES)
            row = jnp.broadcast_to(u_ref[pl.ds(b, 1), :], (LANES, LANES))
            scale = jnp.broadcast_to(
                jnp.sum(jnp.where(eye, row, 0.0), axis=1, keepdims=True), (LANES, LANES)
            )
            for c in range(fr):
                part = e_ref[spot, c * LANES : (c + 1) * LANES].astype(jnp.float32) * scale
                col_ref[c] += jnp.sum(part.reshape(LANES // 8, 8, LANES), axis=0)
            return carry

        lax.fori_loop(0, wr, block, 0)
        msg_f[turn, :fr, :] = jnp.sum(col_ref[...], axis=1)

    def judge(total, peak):
        least = jnp.min(total)
        most = jnp.max(total)
        good = (least > LEAST) & (most < MOST)
        fine = jnp.where(good, least, -1.0)
        return jnp.where(peak * TINY <= fine, 0.0, 1.0)

    for turn in range(ITERS):
        if turn == 0:
            biggest = jnp.ones((8, LANES), jnp.float32)
        else:
            row_pass(turn, scale)
            biggest = jnp.full((8, LANES), jnp.max(v_ref[...]), jnp.float32)
        msg_w[turn, wr:, :] = jnp.where(fault > 0.5, infinite, biggest)
        copies = exchange(turn, msg_w, in_w, send_w, recv_w, af_size, True)
        weights = None
        if turn == 0:
            finish(exchange(0, msg_m, in_m, send_m, recv_m, af_size, True))
            peaks = [arrival(0, msg_m, in_m, af_size, af, k) for k in range(af_size)]
            top = functools.reduce(jnp.maximum, peaks)
            weights = [jnp.exp(p - top) for p in peaks]
            scale = jnp.exp(msg_m[0] - top)
        finish(copies)
        total, peak = ordered(turn, msg_w, in_w, af_size, af, wr, weights)
        fault = judge(total, peak)
        u = wmass_ref[...] / total
        u_ref[...] = u * scale
        if turn == ITERS - 1:
            wsum_ref[...] = jnp.log(total) + top
        col_pass(turn)
        least_u = jnp.full((8, LANES), jnp.min(u), jnp.float32)
        spoiled = (fault > 0.5) | (least_u < 1e-35)
        msg_f[turn, fr:, :] = jnp.where(
            spoiled, infinite, jnp.full((8, LANES), jnp.max(u), jnp.float32)
        )
        finish(exchange(turn, msg_f, in_f, send_f, recv_f, wa_size, False))
        total, peak = ordered(turn, msg_f, in_f, wa_size, wa, fr)
        fault = judge(total, peak)
        v_ref[...] = fmass_ref[...] / total
        if turn == ITERS - 1:
            fsum_ref[...] = jnp.log(total)
    msg_b[0] = fault
    finish(exchange(0, msg_b, in_b, send_b, recv_b, af_size, True))
    for d in range(1, af_size):
        fault = jnp.maximum(fault, in_b[d - 1])
    bad_ref[...] = fault


def fast_sweeps(projected, firm_rows, worker_mass, firm_mass):
    wa_size, af_size = lax.axis_size("wa"), lax.axis_size("af")
    wt, ft = projected.shape[0], firm_rows.shape[0]
    wr, fr = wt // LANES, ft // LANES
    vmem = pl.BlockSpec(memory_space=pltpu.VMEM)
    f32 = jnp.float32
    return pl.pallas_call(
        functools.partial(sweep_kernel, wa_size, af_size),
        out_shape=(
            jax.ShapeDtypeStruct((wr, LANES), f32),
            jax.ShapeDtypeStruct((fr, LANES), f32),
            jax.ShapeDtypeStruct((8, LANES), f32),
        ),
        in_specs=[vmem] * 4,
        out_specs=(vmem, vmem, vmem),
        scratch_shapes=[
            pltpu.VMEM((wt, ft), jnp.bfloat16),
            pltpu.VMEM((256, ft), f32),
            pltpu.VMEM((fr, LANES), f32),
            pltpu.VMEM((wr, LANES), f32),
            pltpu.VMEM((fr, 8, LANES), f32),
            pltpu.VMEM((ITERS, wr + 8, LANES), f32),
            pltpu.VMEM((ITERS, fr + 8, LANES), f32),
            pltpu.VMEM((1, 8, LANES), f32),
            pltpu.VMEM((1, wr, LANES), f32),
            pltpu.VMEM((ITERS * (af_size - 1), wr + 8, LANES), f32),
            pltpu.VMEM((ITERS * (wa_size - 1), fr + 8, LANES), f32),
            pltpu.VMEM((af_size - 1, 8, LANES), f32),
            pltpu.VMEM((af_size - 1, wr, LANES), f32),
            pltpu.SemaphoreType.DMA((ITERS * (af_size - 1),)),
            pltpu.SemaphoreType.DMA((ITERS * (af_size - 1),)),
            pltpu.SemaphoreType.DMA((ITERS * (wa_size - 1),)),
            pltpu.SemaphoreType.DMA((ITERS * (wa_size - 1),)),
            pltpu.SemaphoreType.DMA((af_size - 1,)),
            pltpu.SemaphoreType.DMA((af_size - 1,)),
            pltpu.SemaphoreType.DMA((af_size - 1,)),
            pltpu.SemaphoreType.DMA((af_size - 1,)),
        ],
        compiler_params=pltpu.CompilerParams(
            collective_id=0, has_side_effects=True, vmem_limit_bytes=VMEM_BYTES
        ),
        name="sweeps",
    )(projected, firm_rows.T, worker_mass.reshape(wr, LANES), firm_mass.reshape(fr, LANES))


def body(worker_ids, worker_attrs, firm_ids, firm_attrs, affinity):
    rows = worker_ids.shape[0]
    wa_count = lax.axis_size("wa")
    af_count = lax.axis_size("af")
    worker_tile = W // wa_count
    firm_tile = F // af_count
    records_all = rows * wa_count * af_count
    sent_attrs, sent_ids = pack_records(
        worker_ids, worker_attrs, worker_tile, wa_count, 2 * rows // wa_count
    )
    recv_attrs = lax.all_to_all(sent_attrs, "wa", split_axis=0, concat_axis=0, tiled=True)
    recv_ids = lax.all_to_all(sent_ids, "wa", split_axis=0, concat_axis=0, tiled=True)
    worker_sum, worker_tally = pool_records(recv_attrs, recv_ids, worker_tile)
    sent_attrs, sent_ids = pack_records(
        firm_ids, firm_attrs, firm_tile, af_count, 2 * rows // af_count
    )
    recv_attrs = lax.all_to_all(sent_attrs, "af", split_axis=0, concat_axis=0, tiled=True)
    recv_ids = lax.all_to_all(sent_ids, "af", split_axis=0, concat_axis=0, tiled=True)
    firm_sum, firm_tally = pool_records(recv_attrs, recv_ids, firm_tile)
    worker_means, worker_tally = shared_means(worker_sum, worker_tally, "af")
    firm_means, firm_tally = shared_means(firm_sum, firm_tally, "wa")
    log_worker = jnp.log(worker_tally + 1.0) - jnp.log(jnp.float32(records_all + W))
    log_firm = jnp.log(firm_tally + 1.0) - jnp.log(jnp.float32(records_all + F))
    projected = jnp.dot(
        worker_means.astype(jnp.bfloat16), affinity, preferred_element_type=jnp.float32
    ).astype(jnp.bfloat16)
    firm_rows = firm_means.astype(jnp.bfloat16)
    worker_total, firm_total, bad = fast_sweeps(
        projected,
        firm_rows,
        (worker_tally + 1.0) / jnp.float32(records_all + W),
        (firm_tally + 1.0) / jnp.float32(records_all + F),
    )
    worker_potential, firm_potential = lax.cond(
        bad[0, 0] > 0.5,
        lambda: log_sweeps(projected, firm_rows, log_worker, log_firm),
        lambda: (
            log_worker - worker_total.reshape(-1),
            log_firm - firm_total.reshape(-1),
        ),
    )
    return (
        worker_means,
        firm_means,
        worker_potential,
        firm_potential,
    )


def solution(mesh):
    placed = (P(("wa", "af")), P(("wa", "af"), None), P(("wa", "af")), P(("wa", "af"), None), P())
    return jax.shard_map(
        body,
        mesh=mesh,
        in_specs=placed,
        out_specs=(P("wa", None), P("af", None), P("wa"), P("af")),
        check_vma=False,
    )
```

```python
import functools
import math

import jax
import jax.numpy as jnp
from jax import lax
from jax.experimental import pallas as pl
from jax.experimental.pallas import tpu as pltpu
from jax.sharding import PartitionSpec as P

W = 32768
F = 16384
ITERS = 3
LANES = 128
VMEM_BYTES = 60 * 1024 * 1024
MESH = pl.DeviceIdType.MESH


def select_kernel(chunk, wide, used_ref, low_ref, sec_ref, attrs_ref, after_ref, out_ref, rhs_ref, sum_ref):
    rows, width = attrs_ref.shape
    block = out_ref.shape[1]
    step = pl.program_id(0)

    @pl.when(step == 0)
    def _():
        eye = lax.broadcasted_iota(jnp.int32, (LANES, LANES), 0) == lax.broadcasted_iota(
            jnp.int32, (LANES, LANES), 1
        )

        def fill(c, carry):
            sec_row = jnp.broadcast_to(sec_ref[pl.ds(c, 1), :], (LANES, LANES))
            sec_col = jnp.sum(jnp.where(eye, sec_row, 0.0), axis=1, keepdims=True)
            spot = pl.ds(pl.multiple_of(c * LANES, LANES), LANES)
            part = attrs_ref[spot, :].astype(jnp.float32)
            for s in range(wide):
                rhs_ref[spot, s * width : (s + 1) * width] = jnp.where(
                    sec_col == s, part, 0.0
                ).astype(jnp.bfloat16)
            return carry

        lax.fori_loop(0, rows // LANES, fill, 0)

    target = lax.broadcasted_iota(jnp.int32, (block, chunk), 0) + step * block
    sum_ref[...] = jnp.zeros_like(sum_ref)
    for c in range(rows // chunk):

        @pl.when(used_ref[c] > 0)
        def _(c=c):
            hit = jnp.where(low_ref[c : c + 1, :] == target, 1.0, 0.0).astype(jnp.bfloat16)
            sum_ref[...] += jnp.dot(
                hit, rhs_ref[c * chunk : (c + 1) * chunk, :], preferred_element_type=jnp.float32
            )

    for s in range(wide):
        out_ref[s] = sum_ref[:, s * width : (s + 1) * width].astype(out_ref.dtype)


def select_sum(ids, attrs, count, dtype, after):
    rows, width = attrs.shape
    wide = 2
    span = count // wide
    block = math.gcd(span, 256)
    chunk = math.gcd(rows, 512)
    used = jnp.any(ids.reshape(rows // chunk, chunk) < count, axis=1).astype(jnp.int32)
    sec = ids // span
    low = (ids - sec * span).reshape(rows // chunk, chunk)
    sec = sec.astype(jnp.float32).reshape(rows // LANES, LANES)
    whole = lambda shape: pl.BlockSpec(shape, lambda i: (0,) * len(shape))
    out = pl.pallas_call(
        functools.partial(select_kernel, chunk, wide),
        grid=(span // block,),
        out_shape=jax.ShapeDtypeStruct((wide, span, width), dtype),
        in_specs=[
            pl.BlockSpec(memory_space=pltpu.SMEM),
            whole(low.shape),
            whole(sec.shape),
            whole(attrs.shape),
            pl.BlockSpec(memory_space=pl.ANY),
        ],
        out_specs=pl.BlockSpec((wide, block, width), lambda i: (0, i, 0)),
        scratch_shapes=[
            pltpu.VMEM((rows, wide * width), jnp.bfloat16),
            pltpu.VMEM((block, wide * width), jnp.float32),
        ],
        compiler_params=pltpu.CompilerParams(vmem_limit_bytes=VMEM_BYTES),
        cost_estimate=pl.CostEstimate(
            flops=2 * rows * count * width, bytes_accessed=rows * width * 4, transcendentals=0
        ),
        name="select_sum",
    )(used, low, sec, attrs, after)
    return out.reshape(count, width)


def pack_records(type_ids, attrs, tile, groups, capacity, after):
    rows = type_ids.shape[0]
    owner = type_ids // tile
    local = type_ids - owner * tile
    grid = owner.reshape(rows // LANES, LANES)
    hits = (grid[None] == jnp.arange(groups, dtype=jnp.int32)[:, None, None])
    ramp = jnp.arange(LANES, dtype=jnp.int32)
    upper = (ramp[:, None] <= ramp[None, :]).astype(jnp.bfloat16)
    within = jnp.dot(hits.astype(jnp.bfloat16), upper, preferred_element_type=jnp.float32)
    lines = within[:, :, -1]
    line = jnp.arange(rows // LANES, dtype=jnp.int32)
    before = jnp.sum(
        jnp.where(line[None, :, None] < line[None, None, :], lines[:, :, None], 0.0), axis=1
    )
    rank = jnp.sum(jnp.where(hits, within - 1.0 + before[:, :, None], 0.0), axis=0)
    place = (grid * capacity + rank.astype(jnp.int32)).reshape(rows)
    sent_attrs = select_sum(place, attrs, groups * capacity, jnp.bfloat16, after)
    high, lowd = local // 64, local % 64
    chosen = place_ids(place, jnp.stack([high, lowd, jnp.ones_like(high)]), groups, capacity)
    chosen = chosen.reshape(3, groups, capacity // LANES, LANES)
    high = jnp.where(chosen[2] > 0.5, chosen[0], float(tile // 64))
    sent_attrs = sent_attrs.reshape(groups, capacity, attrs.shape[1])
    return jnp.concatenate(
        [sent_attrs, high.astype(jnp.bfloat16), chosen[1].astype(jnp.bfloat16)], axis=1
    )


def place_ids(place, digits, groups, capacity):
    slots = groups * capacity
    high, low = place // LANES, place % LANES
    ahead = (high[None, :] == jnp.arange(slots // LANES, dtype=jnp.int32)[:, None])
    behind = (low[None, :] == jnp.arange(LANES, dtype=jnp.int32)[:, None]).astype(jnp.bfloat16)
    out = []
    for d in range(digits.shape[0]):
        left = jnp.where(ahead, digits[d][None, :].astype(jnp.bfloat16), jnp.bfloat16(0))
        out.append(
            lax.dot_general(left, behind, (((1,), (1,)), ((), ())), preferred_element_type=jnp.float32)
        )
    return jnp.stack(out).reshape(digits.shape[0], slots)


def pool_records(recv_attrs, recv_ids, tile, after):
    width = recv_attrs.shape[2]
    flat_ids = recv_ids.reshape(-1)
    totals = select_sum(flat_ids, recv_attrs.reshape(-1, width), tile, jnp.float32, after)
    high, low = flat_ids // LANES, flat_ids % LANES
    ahead = (high[None, :] == jnp.arange(tile // LANES, dtype=jnp.int32)[:, None])
    behind = (low[None, :] == jnp.arange(LANES, dtype=jnp.int32)[:, None])
    tallies = lax.dot_general(
        ahead.astype(jnp.bfloat16),
        behind.astype(jnp.bfloat16),
        (((1,), (1,)), ((), ())),
        preferred_element_type=jnp.float32,
    )
    return jnp.concatenate([totals, tallies.reshape(tile // width, width)], axis=0)


def moved(sent, axis, capacity):
    got = lax.all_to_all(sent, axis, split_axis=0, concat_axis=0, tiled=True)
    lines = capacity // LANES
    high = got[:, capacity : capacity + lines].astype(jnp.int32)
    low = got[:, capacity + lines :].astype(jnp.int32)
    return (got[:, :capacity], high * 64 + low)


def shared_means(both, tile, axis):
    both = lax.psum(both, axis)
    tally = both[tile:].reshape(tile)
    return (both[:tile] / jnp.maximum(tally, 1.0)[:, None], tally)


def joined(value, axis, combine):
    everything = jax.tree.map(lambda part: lax.all_gather(part, axis), value)
    initial = jax.tree.map(lambda part: part[0], everything)

    def step(k, so_far):
        return combine(so_far, jax.tree.map(lambda part: part[k], everything))

    return lax.fori_loop(1, lax.axis_size(axis), step, initial)


def merge_pair(left, right):
    peak = jnp.maximum(left[0], right[0])
    return (peak, left[1] * jnp.exp(left[0] - peak) + right[1] * jnp.exp(right[0] - peak))


def log_sweeps(projected, firm_rows, log_worker, log_firm):
    worker_tile, firm_tile = projected.shape[0], firm_rows.shape[0]
    height = math.gcd(worker_tile, 512)
    blocks = worker_tile // height

    def surplus(index):
        rows_block = lax.dynamic_slice_in_dim(projected, index * height, height, 0)
        return jnp.dot(rows_block, firm_rows.T, preferred_element_type=jnp.float32)

    def sweep(rounds, carry):
        firm_potential = carry[1]

        def row_stats(index):
            scores = surplus(index) + firm_potential[None, :]
            peak = jnp.max(scores, axis=1)
            return (peak, jnp.sum(jnp.exp(scores - peak[:, None]), axis=1))

        peak, total = lax.map(row_stats, jnp.arange(blocks, dtype=jnp.int32))
        peak, total = joined((peak.reshape(-1), total.reshape(-1)), "af", merge_pair)
        worker_potential = log_worker - (peak + jnp.log(total))

        def col_step(carry, inputs):
            peak, total = carry
            index, shift_block = inputs
            scores = surplus(index) + shift_block[:, None]
            new_peak = jnp.maximum(peak, jnp.max(scores, axis=0))
            total = total * jnp.exp(peak - new_peak) + jnp.sum(
                jnp.exp(scores - new_peak[None, :]), axis=0
            )
            return ((new_peak, total), None)

        start = (
            jnp.full((firm_tile,), -jnp.inf, jnp.float32),
            jnp.zeros((firm_tile,), jnp.float32),
        )
        (peak, total), _ = lax.scan(
            col_step,
            start,
            (jnp.arange(blocks, dtype=jnp.int32), worker_potential.reshape(blocks, height)),
        )
        peak, total = joined((peak, total), "wa", merge_pair)
        return (worker_potential, log_firm - (peak + jnp.log(total)))

    start = (jnp.zeros((worker_tile,), jnp.float32), jnp.zeros((firm_tile,), jnp.float32))
    return lax.fori_loop(0, ITERS, sweep, start)


TINY = 4e-28
LEAST = 1e-25
MOST = 1e30


def sweep_kernel(
    wa_size, af_size, proj_ref, firm_ref, wmass_ref, fmass_ref,
    wsum_ref, fsum_ref, bad_ref,
    e_ref, s_ref, v_ref, u_ref, col_ref, msg_w, msg_f, msg_b, msg_m, in_w, in_f, in_b, in_m,
    send_w, recv_w, send_f, recv_f, send_b, recv_b, send_m, recv_m,
):
    wa, af = lax.axis_index("wa"), lax.axis_index("af")
    wt, ft = proj_ref.shape[0], firm_ref.shape[1]
    wr, fr = wt // LANES, ft // LANES

    barrier = pltpu.get_barrier_semaphore()
    for d in range(1, af_size):
        pl.semaphore_signal(
            barrier, inc=1, device_id=(wa, lax.rem(af + d, af_size)), device_id_type=MESH
        )
    for d in range(1, wa_size):
        pl.semaphore_signal(
            barrier, inc=1, device_id=(lax.rem(wa + d, wa_size), af), device_id_type=MESH
        )

    eye = lax.broadcasted_iota(jnp.int32, (LANES, LANES), 0) == lax.broadcasted_iota(
        jnp.int32, (LANES, LANES), 1
    )

    def lay(column):
        return jnp.sum(jnp.where(eye, column, 0.0), axis=0, keepdims=True)

    def exchange(turn, msg, inbox, send, recv, size, along_af):
        copies = []
        for d in range(1, size):
            if along_af:
                peer = (wa, lax.rem(af + d, size))
            else:
                peer = (lax.rem(wa + d, size), af)
            slot = turn * (size - 1) + d - 1
            copies.append(
                pltpu.make_async_remote_copy(
                    src_ref=msg.at[turn],
                    dst_ref=inbox.at[slot],
                    send_sem=send.at[slot],
                    recv_sem=recv.at[slot],
                    device_id=peer,
                    device_id_type=MESH,
                )
            )
        for copy in copies:
            copy.start()
        return copies

    def finish(copies):
        for copy in copies:
            copy.wait()

    def arrival(turn, msg, inbox, size, me, k):
        d = lax.rem(me - k + size, size)
        slot = turn * (size - 1) + jnp.maximum(d - 1, 0)
        return jnp.where(d == 0, msg[turn], inbox[slot])

    def ordered(turn, msg, inbox, size, me, rows, weights=None):
        total = jnp.zeros((rows, LANES), jnp.float32)
        peak = jnp.zeros((8, LANES), jnp.float32)
        for k in range(size):
            value = arrival(turn, msg, inbox, size, me, k)
            part = value[:rows]
            if weights is not None:
                part = part * weights[k]
            total = total + part
            peak = jnp.maximum(peak, value[rows:])
        return total, peak

    def fill(b, carry):
        spot = pl.ds(pl.multiple_of(b * 256, 256), 256)
        peak = jnp.full((256, LANES), -jnp.inf, jnp.float32)
        for c in range(ft // 512):
            scores = jnp.dot(
                proj_ref[spot, :],
                firm_ref[:, c * 512 : (c + 1) * 512],
                preferred_element_type=jnp.float32,
            )
            s_ref[:, c * 512 : (c + 1) * 512] = scores
            for k in range(4):
                peak = jnp.maximum(peak, scores[:, k * LANES : (k + 1) * LANES])
        peak = jnp.max(peak, axis=1, keepdims=True)
        shift = jnp.broadcast_to(peak, (256, LANES))
        acc = jnp.zeros((256, LANES), jnp.float32)
        for c in range(fr):
            grown = jnp.exp(s_ref[:, c * LANES : (c + 1) * LANES] - shift)
            e_ref[spot, c * LANES : (c + 1) * LANES] = grown.astype(jnp.bfloat16)
            acc = acc + grown
        total = jnp.sum(acc, axis=1, keepdims=True)
        for k in range(2):
            part = slice(k * LANES, (k + 1) * LANES)
            msg_w[0, pl.ds(b * 2 + k, 1), :] = lay(total[part])
            msg_m[0, pl.ds(b * 2 + k, 1), :] = lay(peak[part])
        return carry

    lax.fori_loop(0, wt // 256, fill, 0)
    pl.semaphore_wait(barrier, af_size + wa_size - 2)

    fault = jnp.zeros((8, LANES), jnp.float32)
    infinite = jnp.full((8, LANES), jnp.inf, jnp.float32)

    def row_pass(turn, scale):
        def block(b, carry):
            spot = pl.ds(pl.multiple_of(b * LANES, LANES), LANES)
            acc = jnp.zeros((LANES, LANES), jnp.float32)
            for c in range(fr):
                acc = acc + e_ref[spot, c * LANES : (c + 1) * LANES].astype(
                    jnp.float32
                ) * v_ref[c : c + 1, :]
            msg_w[turn, pl.ds(b, 1), :] = lay(jnp.sum(acc, axis=1, keepdims=True))
            return carry

        lax.fori_loop(0, wr, block, 0)
        msg_w[turn, :wr, :] = msg_w[turn, :wr, :] * scale

    def col_pass(turn):
        col_ref[...] = jnp.zeros_like(col_ref)

        def block(b, carry):
            spot = pl.ds(pl.multiple_of(b * LANES, LANES), LANES)
            row = jnp.broadcast_to(u_ref[pl.ds(b, 1), :], (LANES, LANES))
            scale = jnp.broadcast_to(
                jnp.sum(jnp.where(eye, row, 0.0), axis=1, keepdims=True), (LANES, LANES)
            )
            for c in range(fr):
                part = e_ref[spot, c * LANES : (c + 1) * LANES].astype(jnp.float32) * scale
                col_ref[c] += jnp.sum(part.reshape(LANES // 8, 8, LANES), axis=0)
            return carry

        lax.fori_loop(0, wr, block, 0)
        msg_f[turn, :fr, :] = jnp.sum(col_ref[...], axis=1)

    def judge(total, peak):
        least = jnp.min(total)
        most = jnp.max(total)
        good = (least > LEAST) & (most < MOST)
        fine = jnp.where(good, least, -1.0)
        return jnp.where(peak * TINY <= fine, 0.0, 1.0)

    for turn in range(ITERS):
        if turn == 0:
            biggest = jnp.ones((8, LANES), jnp.float32)
        else:
            row_pass(turn, scale)
            biggest = jnp.full((8, LANES), jnp.max(v_ref[...]), jnp.float32)
        msg_w[turn, wr:, :] = jnp.where(fault > 0.5, infinite, biggest)
        copies = exchange(turn, msg_w, in_w, send_w, recv_w, af_size, True)
        weights = None
        if turn == 0:
            finish(exchange(0, msg_m, in_m, send_m, recv_m, af_size, True))
            peaks = [arrival(0, msg_m, in_m, af_size, af, k) for k in range(af_size)]
            top = functools.reduce(jnp.maximum, peaks)
            weights = [jnp.exp(p - top) for p in peaks]
            scale = jnp.exp(msg_m[0] - top)
        finish(copies)
        total, peak = ordered(turn, msg_w, in_w, af_size, af, wr, weights)
        fault = judge(total, peak)
        u = wmass_ref[...] / total
        u_ref[...] = u * scale
        if turn == ITERS - 1:
            wsum_ref[...] = jnp.log(total) + top
        col_pass(turn)
        least_u = jnp.full((8, LANES), jnp.min(u), jnp.float32)
        spoiled = (fault > 0.5) | (least_u < 1e-35)
        msg_f[turn, fr:, :] = jnp.where(
            spoiled, infinite, jnp.full((8, LANES), jnp.max(u), jnp.float32)
        )
        finish(exchange(turn, msg_f, in_f, send_f, recv_f, wa_size, False))
        total, peak = ordered(turn, msg_f, in_f, wa_size, wa, fr)
        fault = judge(total, peak)
        v_ref[...] = fmass_ref[...] / total
        if turn == ITERS - 1:
            fsum_ref[...] = jnp.log(total)
    msg_b[0] = fault
    finish(exchange(0, msg_b, in_b, send_b, recv_b, af_size, True))
    for d in range(1, af_size):
        fault = jnp.maximum(fault, in_b[d - 1])
    bad_ref[...] = fault


def fast_sweeps(projected, firm_rows, worker_mass, firm_mass):
    wa_size, af_size = lax.axis_size("wa"), lax.axis_size("af")
    wt, ft = projected.shape[0], firm_rows.shape[0]
    wr, fr = wt // LANES, ft // LANES
    vmem = pl.BlockSpec(memory_space=pltpu.VMEM)
    f32 = jnp.float32
    return pl.pallas_call(
        functools.partial(sweep_kernel, wa_size, af_size),
        out_shape=(
            jax.ShapeDtypeStruct((wr, LANES), f32),
            jax.ShapeDtypeStruct((fr, LANES), f32),
            jax.ShapeDtypeStruct((8, LANES), f32),
        ),
        in_specs=[vmem] * 4,
        out_specs=(vmem, vmem, vmem),
        scratch_shapes=[
            pltpu.VMEM((wt, ft), jnp.bfloat16),
            pltpu.VMEM((256, ft), f32),
            pltpu.VMEM((fr, LANES), f32),
            pltpu.VMEM((wr, LANES), f32),
            pltpu.VMEM((fr, 8, LANES), f32),
            pltpu.VMEM((ITERS, wr + 8, LANES), f32),
            pltpu.VMEM((ITERS, fr + 8, LANES), f32),
            pltpu.VMEM((1, 8, LANES), f32),
            pltpu.VMEM((1, wr, LANES), f32),
            pltpu.VMEM((ITERS * (af_size - 1), wr + 8, LANES), f32),
            pltpu.VMEM((ITERS * (wa_size - 1), fr + 8, LANES), f32),
            pltpu.VMEM((af_size - 1, 8, LANES), f32),
            pltpu.VMEM((af_size - 1, wr, LANES), f32),
            pltpu.SemaphoreType.DMA((ITERS * (af_size - 1),)),
            pltpu.SemaphoreType.DMA((ITERS * (af_size - 1),)),
            pltpu.SemaphoreType.DMA((ITERS * (wa_size - 1),)),
            pltpu.SemaphoreType.DMA((ITERS * (wa_size - 1),)),
            pltpu.SemaphoreType.DMA((af_size - 1,)),
            pltpu.SemaphoreType.DMA((af_size - 1,)),
            pltpu.SemaphoreType.DMA((af_size - 1,)),
            pltpu.SemaphoreType.DMA((af_size - 1,)),
        ],
        compiler_params=pltpu.CompilerParams(
            collective_id=0, has_side_effects=True, vmem_limit_bytes=VMEM_BYTES
        ),
        name="sweeps",
    )(projected, firm_rows.T, worker_mass.reshape(wr, LANES), firm_mass.reshape(fr, LANES))


def body(worker_ids, worker_attrs, firm_ids, firm_attrs, affinity):
    rows = worker_ids.shape[0]
    wa_count = lax.axis_size("wa")
    af_count = lax.axis_size("af")
    worker_tile = W // wa_count
    firm_tile = F // af_count
    records_all = rows * wa_count * af_count
    worker_sent = pack_records(
        worker_ids, worker_attrs, worker_tile, wa_count, 2 * rows // wa_count, affinity
    )
    worker_got = moved(worker_sent, "wa", 2 * rows // wa_count)
    firm_sent = pack_records(
        firm_ids, firm_attrs, firm_tile, af_count, 2 * rows // af_count, worker_sent
    )
    firm_got = moved(firm_sent, "af", 2 * rows // af_count)
    firm_both = pool_records(*firm_got, firm_tile, affinity)
    firm_means, firm_tally = shared_means(firm_both, firm_tile, "wa")
    worker_both = pool_records(*worker_got, worker_tile, affinity)
    worker_means, worker_tally = shared_means(worker_both, worker_tile, "af")
    log_worker = jnp.log(worker_tally + 1.0) - jnp.log(jnp.float32(records_all + W))
    log_firm = jnp.log(firm_tally + 1.0) - jnp.log(jnp.float32(records_all + F))
    projected = jnp.dot(
        worker_means.astype(jnp.bfloat16), affinity, preferred_element_type=jnp.float32
    ).astype(jnp.bfloat16)
    firm_rows = firm_means.astype(jnp.bfloat16)
    worker_total, firm_total, bad = fast_sweeps(
        projected,
        firm_rows,
        (worker_tally + 1.0) / jnp.float32(records_all + W),
        (firm_tally + 1.0) / jnp.float32(records_all + F),
    )
    worker_potential, firm_potential = lax.cond(
        bad[0, 0] > 0.5,
        lambda: log_sweeps(projected, firm_rows, log_worker, log_firm),
        lambda: (
            log_worker - worker_total.reshape(-1),
            log_firm - firm_total.reshape(-1),
        ),
    )
    return (
        worker_means,
        firm_means,
        worker_potential,
        firm_potential,
    )


def solution(mesh):
    placed = (P(("wa", "af")), P(("wa", "af"), None), P(("wa", "af")), P(("wa", "af"), None), P())
    return jax.shard_map(
        body,
        mesh=mesh,
        in_specs=placed,
        out_specs=(P("wa", None), P("af", None), P("wa"), P("af")),
        check_vma=False,
    )
```
